1024 devices in a mesh: ctx: 32 (over x_lo, z), dp: 32 (over y, x_hi, core).
Axes of the slice: x: 4 (x_hi: 2, x_lo: 2; x = x_hi * 2 + x_lo), y: 8, z: 16, core: 2. Of those that a mesh axis runs over, the one named last changes fastest.
Arguments:
- query: bfloat16 [32, 4096, 1024], P('dp', 'ctx'), may hold values from -6 to 6
- key_in: bfloat16 [32, 4096, 1024], P('dp', 'ctx'), may hold values from -6 to 6
- value: bfloat16 [32, 4096, 1024], P('dp', 'ctx'), may hold values from -6 to 6
- cotangent: bfloat16 [32, 4096, 1024], P('dp', 'ctx'), may hold values from -6 to 6
- filters: bfloat16 [32, 4096], P('ctx'), may hold values from -0.09375 to 0.09375
Outputs:
- output: bfloat16 [32, 4096, 1024], P('dp', 'ctx')
- grad_query: bfloat16 [32, 4096, 1024], P('dp', 'ctx')
- grad_key: bfloat16 [32, 4096, 1024], P('dp', 'ctx')
- grad_value: bfloat16 [32, 4096, 1024], P('dp', 'ctx')
- grad_filter: float32 [32, 4096], P('ctx', 'dp')
The draws below stay inside these ranges and needn't reach their ends.
All inputs are finite; a program needn't handle non-finite values.
Results may differ from the reference program's by a relative error of at most 0.0058.
Values may be sent and summed in bfloat16 or wider, within the bound.
No kernel may reach another device: no remote copies, remote signals or barrier semaphores. Data moves between devices by JAX's collectives and lax.ppermute only.
A program may use at most 64 MiB of HBM per device.

```python
import math
import jax
import jax.numpy as jnp
from jax import lax

C = 1024
CPG = 32
BLK = 256
LENGTH = 4096
BATCH = 32
GROUPS = 32


def steps_of(key, extent, pieces, least, largest):
    factor_of, own = 1.0, jax.random.fold_in(key, 6)
    for axis_at, parts in pieces:
        heights = jnp.exp(jax.random.uniform(jax.random.fold_in(own, axis_at), (parts,), jnp.float32, least / len(pieces), largest / len(pieces)))
        factor_of = factor_of * jnp.repeat(heights, extent[axis_at] // parts).reshape([-1 if axis == axis_at else 1 for axis in range(len(extent))])
    return factor_of


def gaussian(rng, dims, deviation, limit, cuts=(), held_as=jnp.bfloat16):
    loudness = steps_of(rng, dims, cuts, -0.22, 0.18) if cuts else 1.0
    values = jax.random.normal(rng, dims, jnp.float32) * deviation * loudness
    return jnp.minimum(jnp.maximum(values, -limit), limit).astype(held_as)


def setup_inputs(seed: int = 0) -> dict:
    key_list = jax.random.split(jax.random.key(seed), 6)
    return {
        "query": gaussian(key_list[0], (BATCH, LENGTH, C), 1.0, 6.0, ((0, 32), (1, 32))),
        "key_in": gaussian(key_list[1], (BATCH, LENGTH, C), 1.0, 6.0, ((0, 32), (1, 32))),
        "value": gaussian(key_list[2], (BATCH, LENGTH, C), 1.0, 6.0, ((0, 32), (1, 32))),
        "cotangent": gaussian(key_list[3], (BATCH, LENGTH, C), 1.0, 6.0, ((0, 32), (1, 32))),
        "filters": gaussian(key_list[4], (GROUPS, LENGTH), LENGTH ** -0.5, 0.09375, ((0, 32),)),
    }


def to_blocks(values, blocksize):
    seqcount, length, width = values.shape
    groups = width // CPG
    nblocks = length // blocksize
    arranged = values.reshape(seqcount, nblocks, blocksize, groups, CPG).transpose(3, 2, 1, 0, 4)
    return arranged.reshape(groups, blocksize, nblocks, seqcount * CPG)

def from_blocks(arranged, seqcount):
    groups, blocksize, nblocks, columns = arranged.shape
    values = arranged.reshape(groups, blocksize, nblocks, seqcount, CPG).transpose(3, 2, 1, 0, 4)
    return values.reshape(seqcount, nblocks * blocksize, groups * CPG)

def toeplitz_blocks(filters_local, blocksize):
    groups, length = filters_local.shape
    nblocks = length // blocksize
    extended = jnp.concatenate([jnp.zeros((groups, blocksize - 1), filters_local.dtype), filters_local], axis=1)
    matrices = []
    for offset in range(nblocks):
        window = extended[:, offset * blocksize:offset * blocksize + 2 * blocksize - 1]
        tiled = jnp.tile(window[:, ::-1], (1, blocksize))
        strided = tiled[:, blocksize - 1:blocksize - 1 + blocksize * (2 * blocksize - 2)]
        matrices.append(strided.reshape(groups, blocksize, 2 * blocksize - 2)[:, :, :blocksize])
    return matrices

def conv_forward(matrices, signal):
    groups, blocksize, nblocks, columns = signal.shape
    result = jnp.zeros(signal.shape, jnp.float32)
    for offset, matrix in enumerate(matrices):
        inputs = signal[:, :, :nblocks - offset].reshape(groups, blocksize, (nblocks - offset) * columns)
        partial_out = jnp.einsum('gab,gbw->gaw', matrix.astype(jnp.float32), inputs.astype(jnp.float32))
        partial_out = partial_out.reshape(groups, blocksize, nblocks - offset, columns)
        result = result + jnp.pad(partial_out, ((0, 0), (0, 0), (offset, 0), (0, 0)))
    return result

def conv_adjoint(matrices, grads):
    groups, blocksize, nblocks, columns = grads.shape
    result = jnp.zeros(grads.shape, jnp.float32)
    for offset, matrix in enumerate(matrices):
        outgrad = grads[:, :, offset:].reshape(groups, blocksize, (nblocks - offset) * columns)
        partial_in = jnp.einsum('gab,gaw->gbw', matrix.astype(jnp.float32), outgrad.astype(jnp.float32))
        partial_in = partial_in.reshape(groups, blocksize, nblocks - offset, columns)
        result = result + jnp.pad(partial_in, ((0, 0), (0, 0), (0, offset), (0, 0)))
    return result

def skew_sums(square):
    groups, blocksize, second = square.shape
    padded = jnp.concatenate([square, jnp.zeros_like(square)], axis=2)
    padded = padded.reshape(groups, 2 * blocksize * blocksize)[:, :blocksize * (2 * blocksize - 1)]
    return padded.reshape(groups, blocksize, 2 * blocksize - 1).sum(axis=1)

def filter_terms(grads, signal):
    groups, blocksize, nblocks, columns = signal.shape
    total = jnp.zeros((groups, nblocks * blocksize + blocksize - 1), jnp.float32)
    for offset in range(nblocks):
        outgrad = grads[:, :, offset:].reshape(groups, blocksize, (nblocks - offset) * columns)
        earlier = signal[:, ::-1, :nblocks - offset].reshape(groups, blocksize, (nblocks - offset) * columns)
        flipped = jnp.einsum('gaw,gbw->gab', outgrad.astype(jnp.float32), earlier.astype(jnp.float32))
        total = total + jnp.pad(skew_sums(flipped), ((0, 0), (offset * blocksize, (nblocks - 1 - offset) * blocksize)))
    return total[:, blocksize - 1:]

def reference(query, key_in, value, cotangent, filters):
    mixed = (key_in.astype(jnp.float32) * value.astype(jnp.float32)).astype(jnp.bfloat16)
    gradin = (cotangent.astype(jnp.float32) * query.astype(jnp.float32)).astype(jnp.bfloat16)
    ngroups = C // CPG

    def split(values):
        return values.reshape(BATCH, LENGTH, ngroups, CPG).transpose(2, 0, 1, 3)

    def one_group(operands):
        filt, mixed_group, grad_group = operands
        matrices = toeplitz_blocks(filt[None, :].astype(jnp.float32), BLK)
        signal = to_blocks(mixed_group, BLK)
        grads = to_blocks(grad_group, BLK)
        conv_group = from_blocks(conv_forward(matrices, signal).astype(jnp.bfloat16), BATCH)
        adjoint_group = from_blocks(conv_adjoint(matrices, grads).astype(jnp.bfloat16), BATCH)
        lag_sums = filter_terms(grads, signal)
        return (conv_group, adjoint_group, lag_sums[0])
    conv_all, adjoint_all, lag_all = lax.map(one_group, (filters, split(mixed), split(gradin)))
    conv = conv_all.transpose(1, 2, 0, 3).reshape(BATCH, LENGTH, C)
    adjoint = adjoint_all.transpose(1, 2, 0, 3).reshape(BATCH, LENGTH, C)
    output = (query.astype(jnp.float32) * conv.astype(jnp.float32)).astype(jnp.bfloat16)
    grad_query = (cotangent.astype(jnp.float32) * conv.astype(jnp.float32)).astype(jnp.bfloat16)
    grad_key = (adjoint.astype(jnp.float32) * value.astype(jnp.float32)).astype(jnp.bfloat16)
    grad_value = (adjoint.astype(jnp.float32) * key_in.astype(jnp.float32)).astype(jnp.bfloat16)
    scale_factor = 1.0 / math.sqrt(BATCH * LENGTH * CPG)
    grad_filter = lag_all * jnp.float32(scale_factor)
    return (output, grad_query, grad_key, grad_value, grad_filter)
```

```python
import math

import jax
import jax.numpy as jnp
from jax import lax
from jax.experimental import pallas as pl
from jax.experimental.pallas import tpu as pltpu
from jax.sharding import PartitionSpec as P


CPG = 32
BLK = 256
VMEM = pl.BlockSpec(memory_space=pltpu.VMEM)
F32 = jnp.float32
BF16 = jnp.bfloat16


ANY = pl.BlockSpec(memory_space=pl.ANY)
DMA = pltpu.SemaphoreType.DMA
PARTS = 4


def call(kernel, out_shape, flops, moved, outs=VMEM, limit=16, **kw):
    return pl.pallas_call(
        kernel,
        out_shape=out_shape,
        out_specs=jax.tree.map(lambda _: outs, out_shape),
        cost_estimate=pl.CostEstimate(flops=flops, bytes_accessed=moved, transcendentals=0),
        compiler_params=pltpu.CompilerParams(vmem_limit_bytes=limit * 2**20),
        **kw,
    )


def gate_kernel(k_ref, v_ref, q_ref, g_ref, out_ref, wide_ref, held_ref, in_sem, out_sem):
    groups, _, pos = out_ref.shape
    step = groups // PARTS
    span = step * CPG
    pairs = ((k_ref, v_ref), (g_ref, q_ref))
    loads = []
    for part in range(PARTS):
        at = pl.ds(part * span, span)
        row = [
            [
                pltpu.make_async_copy(
                    ref.at[:, at], wide_ref.at[2 * h + j, :, at], in_sem.at[part, 2 * h + j]
                )
                for j, ref in enumerate(pair)
            ]
            for h, pair in enumerate(pairs)
        ]
        for pair in row:
            for copy in pair:
                copy.start()
        loads.append(row)
    stores = []
    for part in range(PARTS):
        mine = pl.ds(part * step, step)
        for h in range(2):
            for copy in loads[part][h]:
                copy.wait()
            at = slice(part * span, (part + 1) * span)
            one = wide_ref[2 * h, :, at].astype(F32) * wide_ref[2 * h + 1, :, at].astype(F32)
            rows = one.astype(BF16).T.reshape(step, CPG, pos)
            held_ref[part * step : (part + 1) * step, h * CPG : (h + 1) * CPG, :] = rows
        copy = pltpu.make_async_copy(held_ref.at[mine], out_ref.at[mine], out_sem.at[part])
        copy.start()
        stores.append(copy)
    for copy in stores:
        copy.wait()


def band_kernel(f_ref, e_ref):
    length = f_ref.shape[1]
    filt = f_ref[...].astype(F32)
    ext = jnp.concatenate([jnp.zeros((1, BLK), F32), filt], axis=1)
    width = length + BLK
    wide = jnp.broadcast_to(ext, (8, width))
    row = lax.broadcasted_iota(jnp.int32, (8, width), 0)
    base = wide
    for r in range(1, 8):
        base = jnp.where(row == r, pltpu.roll(wide, r, 1), base)
    prev = None
    for q in range(16):
        cur = base if q == 0 else pltpu.roll(base, 8 * q, 1)
        if q % 2 == 0:
            prev = cur
            continue
        pair = jnp.concatenate([prev, cur], axis=0).astype(BF16)
        at = 8 * (q - 1)
        e_ref[at : at + 16, :] = pair[:, BLK:]
        e_ref[128 + at : 128 + at + 16, :] = pair[:, 128 : 128 + length]


def rows_of(ref, half):
    pieces = ref.shape[0]
    part = ref[:, half * CPG : (half + 1) * CPG, :]
    pair = part.reshape(pieces // 2, 2, CPG, 128)
    return jnp.concatenate([pair[:, 0], pair[:, 1]], axis=-1).reshape(pieces // 2 * CPG, BLK)


def put_rows(ref, half, rows):
    pieces = ref.shape[0]
    blocks = rows.reshape(pieces // 2, CPG, BLK)
    both = jnp.stack([blocks[:, :, :128], blocks[:, :, 128:]], axis=1)
    ref[:, half * CPG : (half + 1) * CPG, :] = both.reshape(pieces, CPG, 128)


def conv_kernel(in_ref, e_ref, out_ref, held_ref, x_ref, acc_ref, sem):
    nblocks = in_ref.shape[0] // 2
    x_ref[...] = rows_of(in_ref, 0)
    for d in range(nblocks):
        n = (nblocks - d) * CPG
        part = jnp.dot(
            x_ref[:n, :], e_ref[:, d * BLK : (d + 1) * BLK], preferred_element_type=F32
        )
        if d == 0:
            acc_ref[...] = part
        else:
            acc_ref[d * CPG :, :] += part
    put_rows(held_ref, 0, acc_ref[...].astype(BF16))
    half = pl.ds(0, CPG)
    first = pltpu.make_async_copy(held_ref.at[:, half, :], out_ref.at[:, half, :], sem.at[0])
    first.start()
    x_ref[...] = rows_of(in_ref, 1)
    for d in range(nblocks):
        n = (nblocks - d) * CPG
        part = lax.dot_general(
            x_ref[d * CPG :, :],
            e_ref[:, d * BLK : (d + 1) * BLK],
            (((1,), (1,)), ((), ())),
            preferred_element_type=F32,
        )
        if d == 0:
            acc_ref[...] = part
        else:
            acc_ref[:n, :] += part
    put_rows(held_ref, 1, acc_ref[...].astype(BF16))
    half = pl.ds(CPG, CPG)
    second = pltpu.make_async_copy(held_ref.at[:, half, :], out_ref.at[:, half, :], sem.at[1])
    second.start()
    first.wait()
    second.wait()


def lag_kernel(scale, in_ref, out_ref, xt_ref, g_ref, s_ref):
    nblocks = in_ref.shape[0] // 2
    total = nblocks * CPG
    length = nblocks * BLK
    xt_ref[...] = rows_of(in_ref, 0).T
    g_ref[:total, :] = rows_of(in_ref, 1)
    g_ref[total:, :] = jnp.zeros((128, BLK), BF16)
    s_ref[:, length:] = jnp.zeros((BLK, 128), F32)
    for d in range(nblocks):
        n = -(-(total - d * CPG) // 128) * 128
        s_ref[:, d * BLK : (d + 1) * BLK] = jnp.dot(
            xt_ref[:, :n], g_ref[d * CPG : d * CPG + n, :], preferred_element_type=F32
        )
    width = length + 128
    zeros = jnp.zeros((8, 128), F32)
    acc = None
    for q in range(15, -1, -1):
        low = s_ref[8 * q : 8 * q + 8, :length]
        high = s_ref[128 + 8 * q : 128 + 8 * q + 8, 128:]
        term = jnp.concatenate([low + high, zeros], axis=1)
        acc = term if acc is None else pltpu.roll(acc, width - 8, 1) + term
    row = lax.broadcasted_iota(jnp.int32, (8, width), 0)
    lined = acc
    for r in range(1, 8):
        lined = jnp.where(row == r, pltpu.roll(acc, width - r, 1), lined)
    sums = jnp.sum(lined, axis=0, keepdims=True) * scale
    for i in range(length // 128):
        out_ref[i] = sums[:, 128 * i : 128 * (i + 1)]


def close_kernel(
    in_ref, k_ref, v_ref, q_ref, g_ref, out_ref, gq_ref, gk_ref, gv_ref, held_ref, sem
):
    groups, _, pos = in_ref.shape
    step = groups // PARTS
    span = step * CPG
    copies = []
    for part in range(PARTS):
        at = slice(part * span, (part + 1) * span)
        for h, gates, outs in ((0, (q_ref, g_ref), (out_ref, gq_ref)), (1, (v_ref, k_ref), (gk_ref, gv_ref))):
            rows = in_ref[part * step : (part + 1) * step, h * CPG : (h + 1) * CPG, :]
            wide = rows.reshape(span, pos).T.astype(F32)
            for j in range(2):
                i = 2 * h + j
                held_ref[i, :, at] = (gates[j][:, at].astype(F32) * wide).astype(BF16)
                into = outs[j].at[:, pl.ds(part * span, span)]
                copy = pltpu.make_async_copy(
                    held_ref.at[i, :, pl.ds(part * span, span)], into, sem.at[part, i]
                )
                copy.start()
                copies.append(copy)
    for copy in copies:
        copy.wait()


def halve(terms, replicas):
    me = lax.axis_index("dp")
    bit = replicas // 2
    while bit:
        both = terms.reshape(2, bit, 1, 128)
        high = (me & bit) != 0
        kept = jnp.where(high, both[1], both[0])
        away = jnp.where(high, both[0], both[1])
        got = lax.ppermute(away, "dp", [(i, i ^ bit) for i in range(replicas)])
        terms = kept + got
        bit //= 2
    return terms.reshape(1, 128)


def step(query, key_in, value, cotangent, filters):
    seqcount, pos, channels = query.shape
    groups = channels // CPG
    pieces = lax.axis_size("ctx")
    replicas = lax.axis_size("dp")
    length = pos * pieces
    nblocks = length // BLK
    flat = [a.reshape(pos, channels) for a in (key_in, value, query, cotangent)]
    held = jax.ShapeDtypeStruct((groups, 2 * CPG, pos), BF16)
    size = groups * 2 * CPG * pos * 2
    sent = call(
        gate_kernel,
        held,
        2 * pos * channels,
        3 * size,
        ANY,
        56,
        in_specs=[ANY] * 4,
        scratch_shapes=[
            pltpu.VMEM((4, pos, channels), BF16),
            pltpu.VMEM(held.shape, BF16),
            DMA((PARTS, 4)),
            DMA((PARTS,)),
        ],
        name="gate",
    )(*flat)
    band = call(
        band_kernel,
        jax.ShapeDtypeStruct((BLK, length), BF16),
        BLK * length * 2,
        BLK * length * 2,
        in_specs=[VMEM],
        name="band",
    )(filters)
    owned = lax.all_to_all(sent, "ctx", split_axis=0, concat_axis=0, tiled=True)
    work = 2 * CPG * length * length
    result = call(
        conv_kernel,
        held,
        2 * work,
        2 * size + BLK * length * 2,
        ANY,
        in_specs=[VMEM] * 2,
        scratch_shapes=[
            pltpu.VMEM(held.shape, BF16),
            pltpu.VMEM((nblocks * CPG, BLK), BF16),
            pltpu.VMEM((nblocks * CPG, BLK), F32),
            DMA((2,)),
        ],
        name="conv",
    )(owned, band)
    owned, result = lax.optimization_barrier((owned, result))
    back = lax.all_to_all(result, "ctx", split_axis=0, concat_axis=0, tiled=True)
    scale = 1.0 / math.sqrt(seqcount * replicas * length * CPG)

    def lag_body(*refs):
        lag_kernel(scale, *refs)

    lags_of = call(
        lag_body,
        jax.ShapeDtypeStruct((length // 128, 1, 128), F32),
        work,
        size + BLK * length * 8,
        in_specs=[VMEM],
        scratch_shapes=[
            pltpu.VMEM((BLK, nblocks * CPG), BF16),
            pltpu.VMEM((nblocks * CPG + 128, BLK), BF16),
            pltpu.VMEM((BLK, length + 128), F32),
        ],
        name="lags",
    )
    lags = lags_of(owned)
    grad_filter = halve(lags, replicas)
    wide = jax.ShapeDtypeStruct((pos, channels), BF16)
    outs = call(
        close_kernel,
        (wide,) * 4,
        4 * pos * channels,
        5 * size,
        ANY,
        in_specs=[VMEM] * 5,
        scratch_shapes=[pltpu.VMEM((4, pos, channels), BF16), DMA((PARTS, 4))],
        name="close",
    )(back, *flat)
    return tuple(o.reshape(seqcount, pos, channels) for o in outs) + (grad_filter,)


def solution(mesh):
    spread = P("dp", "ctx", None)
    return jax.shard_map(
        step,
        mesh=mesh,
        in_specs=(spread,) * 4 + (P("ctx", None),),
        out_specs=(spread,) * 4 + (P("ctx", "dp"),),
        check_vma=False,
    )
```

```python
import math

import jax
import jax.numpy as jnp
from jax import lax
from jax.experimental import pallas as pl
from jax.experimental.pallas import tpu as pltpu
from jax.sharding import PartitionSpec as P


CPG = 32
BLK = 256
VMEM = pl.BlockSpec(memory_space=pltpu.VMEM)
F32 = jnp.float32
BF16 = jnp.bfloat16


ANY = pl.BlockSpec(memory_space=pl.ANY)
DMA = pltpu.SemaphoreType.DMA
PARTS = 4


def call(kernel, out_shape, flops, moved, outs, limit=16, **kw):
    return pl.pallas_call(
        kernel,
        out_shape=out_shape,
        out_specs=outs,
        cost_estimate=pl.CostEstimate(flops=flops, bytes_accessed=moved, transcendentals=0),
        compiler_params=pltpu.CompilerParams(vmem_limit_bytes=limit * 2**20),
        **kw,
    )


def gate_kernel(k_ref, v_ref, q_ref, g_ref, out_ref, wide_ref, held_ref, in_sem, out_sem):
    groups, _, pos = out_ref.shape
    step = groups // PARTS
    span = step * CPG
    pairs = ((k_ref, v_ref), (g_ref, q_ref))
    loads = []
    for part in range(PARTS):
        at = pl.ds(part * span, span)
        row = [
            [
                pltpu.make_async_copy(
                    ref.at[:, at], wide_ref.at[2 * h + j, :, at], in_sem.at[part, 2 * h + j]
                )
                for j, ref in enumerate(pair)
            ]
            for h, pair in enumerate(pairs)
        ]
        for pair in row:
            for copy in pair:
                copy.start()
        loads.append(row)
    stores = []
    for part in range(PARTS):
        mine = pl.ds(part * step, step)
        for h in range(2):
            for copy in loads[part][h]:
                copy.wait()
            at = slice(part * span, (part + 1) * span)
            one = wide_ref[2 * h, :, at].astype(F32) * wide_ref[2 * h + 1, :, at].astype(F32)
            rows = one.astype(BF16).T.reshape(step, CPG, pos)
            held_ref[part * step : (part + 1) * step, h * CPG : (h + 1) * CPG, :] = rows
        copy = pltpu.make_async_copy(held_ref.at[mine], out_ref.at[mine], out_sem.at[part])
        copy.start()
        stores.append(copy)
    for copy in stores:
        copy.wait()


def fill_band(taps, e_ref):
    length = taps.shape[1]
    ext = jnp.concatenate([jnp.zeros((1, BLK), F32), taps.astype(F32)], axis=1)
    width = length + BLK
    wide = jnp.broadcast_to(ext, (8, width))
    row = lax.broadcasted_iota(jnp.int32, (8, width), 0)
    base = wide
    for r in range(1, 8):
        base = jnp.where(row == r, pltpu.roll(wide, r, 1), base)
    prev = None
    for q in range(16):
        cur = base if q == 0 else pltpu.roll(base, 8 * q, 1)
        if q % 2 == 0:
            prev = cur
            continue
        pair = jnp.concatenate([prev, cur], axis=0).astype(BF16)
        at = 8 * (q - 1)
        e_ref[at : at + 16, :] = pair[:, BLK:]
        e_ref[128 + at : 128 + at + 16, :] = pair[:, 128 : 128 + length]


def rows_of(ref, half):
    pieces = ref.shape[0]
    part = ref[:, half * CPG : (half + 1) * CPG, :]
    pair = part.reshape(pieces // 2, 2, CPG, 128)
    return jnp.concatenate([pair[:, 0], pair[:, 1]], axis=-1).reshape(pieces // 2 * CPG, BLK)


def put_rows(ref, half, rows):
    pieces = ref.shape[0]
    blocks = rows.reshape(pieces // 2, CPG, BLK)
    both = jnp.stack([blocks[:, :, :128], blocks[:, :, 128:]], axis=1)
    ref[:, half * CPG : (half + 1) * CPG, :] = both.reshape(pieces, CPG, 128)


def conv_kernel(in_ref, f_ref, out_ref, held_ref, e_ref, x_ref, acc_ref, sem):
    fill_band(f_ref[...], e_ref)
    nblocks = in_ref.shape[0] // 2
    x_ref[...] = rows_of(in_ref, 0)
    for d in range(nblocks):
        n = (nblocks - d) * CPG
        part = jnp.dot(
            x_ref[:n, :], e_ref[:, d * BLK : (d + 1) * BLK], preferred_element_type=F32
        )
        if d == 0:
            acc_ref[...] = part
        else:
            acc_ref[d * CPG :, :] += part
    put_rows(held_ref, 0, acc_ref[...].astype(BF16))
    half = pl.ds(0, CPG)
    first = pltpu.make_async_copy(held_ref.at[:, half, :], out_ref.at[:, half, :], sem.at[0])
    first.start()
    x_ref[...] = rows_of(in_ref, 1)
    for d in range(nblocks):
        n = (nblocks - d) * CPG
        part = lax.dot_general(
            x_ref[d * CPG :, :],
            e_ref[:, d * BLK : (d + 1) * BLK],
            (((1,), (1,)), ((), ())),
            preferred_element_type=F32,
        )
        if d == 0:
            acc_ref[...] = part
        else:
            acc_ref[:n, :] += part
    put_rows(held_ref, 1, acc_ref[...].astype(BF16))
    half = pl.ds(CPG, CPG)
    second = pltpu.make_async_copy(held_ref.at[:, half, :], out_ref.at[:, half, :], sem.at[1])
    second.start()
    first.wait()
    second.wait()


def lag_kernel(scale, in_ref, out_ref, me_ref, xt_ref, g_ref, s_ref):
    me_ref[...] = jnp.full(me_ref.shape, lax.axis_index("dp"), jnp.int32)
    nblocks = in_ref.shape[0] // 2
    total = nblocks * CPG
    length = nblocks * BLK
    xt_ref[...] = rows_of(in_ref, 0).T
    g_ref[:total, :] = rows_of(in_ref, 1)
    g_ref[total:, :] = jnp.zeros((128, BLK), BF16)
    s_ref[:, length:] = jnp.zeros((BLK, 128), F32)
    for d in range(nblocks):
        n = -(-(total - d * CPG) // 128) * 128
        s_ref[:, d * BLK : (d + 1) * BLK] = jnp.dot(
            xt_ref[:, :n], g_ref[d * CPG : d * CPG + n, :], preferred_element_type=F32
        )
    width = length + 128
    zeros = jnp.zeros((8, 128), F32)
    acc = None
    for q in range(15, -1, -1):
        low = s_ref[8 * q : 8 * q + 8, :length]
        high = s_ref[128 + 8 * q : 128 + 8 * q + 8, 128:]
        term = jnp.concatenate([low + high, zeros], axis=1)
        acc = term if acc is None else pltpu.roll(acc, width - 8, 1) + term
    row = lax.broadcasted_iota(jnp.int32, (8, width), 0)
    lined = acc
    for r in range(1, 8):
        lined = jnp.where(row == r, pltpu.roll(acc, width - r, 1), lined)
    sums = jnp.sum(lined, axis=0, keepdims=True) * scale
    for i in range(length // 128):
        out_ref[i] = sums[:, 128 * i : 128 * (i + 1)]


def close_kernel(
    in_ref, k_ref, v_ref, q_ref, g_ref, out_ref, gq_ref, gk_ref, gv_ref, held_ref, sem
):
    groups, _, pos = in_ref.shape
    step = groups // PARTS
    span = step * CPG
    copies = []
    for part in range(PARTS):
        at = slice(part * span, (part + 1) * span)
        for h, gates, outs in ((0, (q_ref, g_ref), (out_ref, gq_ref)), (1, (v_ref, k_ref), (gk_ref, gv_ref))):
            rows = in_ref[part * step : (part + 1) * step, h * CPG : (h + 1) * CPG, :]
            wide = rows.reshape(span, pos).T.astype(F32)
            for j in range(2):
                i = 2 * h + j
                held_ref[i, :, at] = (gates[j][:, at].astype(F32) * wide).astype(BF16)
                into = outs[j].at[:, pl.ds(part * span, span)]
                copy = pltpu.make_async_copy(
                    held_ref.at[i, :, pl.ds(part * span, span)], into, sem.at[part, i]
                )
                copy.start()
                copies.append(copy)
    for copy in copies:
        copy.wait()


def halve(terms, me, replicas):
    bit = replicas // 2
    while bit:
        both = terms.reshape(2, bit, 1, 128)
        high = jnp.broadcast_to((me & bit) != 0, (bit, 1, 128))
        kept = jnp.where(high, both[1], both[0])
        away = jnp.where(high, both[0], both[1])
        got = lax.ppermute(away, "dp", [(i, i ^ bit) for i in range(replicas)])
        terms = kept + got
        bit //= 2
    return terms.reshape(1, 128)


def step(query, key_in, value, cotangent, filters):
    seqcount, pos, channels = query.shape
    groups = channels // CPG
    pieces = lax.axis_size("ctx")
    replicas = lax.axis_size("dp")
    length = pos * pieces
    nblocks = length // BLK
    flat = [a.reshape(pos, channels) for a in (key_in, value, query, cotangent)]
    held = jax.ShapeDtypeStruct((groups, 2 * CPG, pos), BF16)
    size = groups * 2 * CPG * pos * 2
    sent = call(
        gate_kernel,
        held,
        2 * pos * channels,
        3 * size,
        ANY,
        56,
        in_specs=[ANY] * 4,
        scratch_shapes=[
            pltpu.VMEM((4, pos, channels), BF16),
            pltpu.VMEM(held.shape, BF16),
            DMA((PARTS, 4)),
            DMA((PARTS,)),
        ],
        name="gate",
    )(*flat)
    owned = lax.all_to_all(sent, "ctx", split_axis=0, concat_axis=0, tiled=True)
    work = 2 * CPG * length * length
    result = call(
        conv_kernel,
        held,
        2 * work,
        2 * size + BLK * length * 2,
        ANY,
        in_specs=[VMEM] * 2,
        scratch_shapes=[
            pltpu.VMEM(held.shape, BF16),
            pltpu.VMEM((BLK, length), BF16),
            pltpu.VMEM((nblocks * CPG, BLK), BF16),
            pltpu.VMEM((nblocks * CPG, BLK), F32),
            DMA((2,)),
        ],
        name="conv",
    )(owned, filters)
    owned, result = lax.optimization_barrier((owned, result))
    back = lax.all_to_all(result, "ctx", split_axis=0, concat_axis=0, tiled=True)
    scale = 1.0 / math.sqrt(seqcount * replicas * length * CPG)

    def lag_body(*refs):
        lag_kernel(scale, *refs)

    lags_of = call(
        lag_body,
        (
            jax.ShapeDtypeStruct((length // 128, 1, 128), F32),
            jax.ShapeDtypeStruct((1, 128), jnp.int32),
        ),
        work,
        size + BLK * length * 8,
        (VMEM, VMEM),
        in_specs=[VMEM],
        scratch_shapes=[
            pltpu.VMEM((BLK, nblocks * CPG), BF16),
            pltpu.VMEM((nblocks * CPG + 128, BLK), BF16),
            pltpu.VMEM((BLK, length + 128), F32),
        ],
        name="lags",
    )
    lags, me = lags_of(owned)
    grad_filter = halve(lags, me, replicas)
    wide = jax.ShapeDtypeStruct((pos, channels), BF16)
    close = call(
        close_kernel,
        (wide,) * 4,
        4 * pos * channels,
        5 * size,
        (ANY,) * 4,
        in_specs=[VMEM] * 5,
        scratch_shapes=[pltpu.VMEM((4, pos, channels), BF16), DMA((PARTS, 4))],
        name="close",
    )
    outs = close(back, *flat)
    return tuple(o.reshape(seqcount, pos, channels) for o in outs) + (grad_filter,)


def solution(mesh):
    spread = P("dp", "ctx", None)
    return jax.shard_map(
        step,
        mesh=mesh,
        in_specs=(spread,) * 4 + (P("ctx", None),),
        out_specs=(spread,) * 4 + (P("ctx", "dp"),),
        check_vma=False,
    )
```

```python
import math

import jax
import jax.numpy as jnp
from jax import lax
from jax.experimental import pallas as pl
from jax.experimental.pallas import tpu as pltpu
from jax.sharding import PartitionSpec as P


CPG = 32
BLK = 256
VMEM = pl.BlockSpec(memory_space=pltpu.VMEM)
F32 = jnp.float32
BF16 = jnp.bfloat16


ANY = pl.BlockSpec(memory_space=pl.ANY)
DMA = pltpu.SemaphoreType.DMA
PARTS = 4


def call(kernel, out_shape, flops, moved, outs, limit=16, **kw):
    return pl.pallas_call(
        kernel,
        out_shape=out_shape,
        out_specs=outs,
        cost_estimate=pl.CostEstimate(flops=flops, bytes_accessed=moved, transcendentals=0),
        compiler_params=pltpu.CompilerParams(vmem_limit_bytes=limit * 2**20),
        **kw,
    )


def gate_kernel(
    k_ref, v_ref, q_ref, g_ref, f_ref, out_ref, e_ref, wide_ref, taps_ref, in_sem, f_sem
):
    groups, _, pos = out_ref.shape
    step = groups // PARTS
    span = step * CPG
    taps = pltpu.make_async_copy(f_ref, taps_ref, f_sem)
    taps.start()
    loads = []
    for part in range(PARTS):
        at = pl.ds(part * span, span)
        row = [
            pltpu.make_async_copy(ref.at[:, at], wide_ref.at[i, :, at], in_sem.at[part, i])
            for i, ref in enumerate((k_ref, v_ref, g_ref, q_ref))
        ]
        for copy in row:
            copy.start()
        loads.append(row)
    taps.wait()
    fill_band(taps_ref[...], e_ref)
    for part in range(PARTS):
        for copy in loads[part]:
            copy.wait()
        at = slice(part * span, (part + 1) * span)
        mine = slice(part * step, (part + 1) * step)
        for h in range(2):
            one = wide_ref[2 * h, :, at].astype(F32) * wide_ref[2 * h + 1, :, at].astype(F32)
            rows = one.astype(BF16).T.reshape(step, CPG, pos)
            out_ref[mine, h * CPG : (h + 1) * CPG, :] = rows


def fill_band(taps, e_ref):
    length = taps.shape[1]
    ext = jnp.concatenate([jnp.zeros((1, BLK), F32), taps.astype(F32)], axis=1)
    width = length + BLK
    wide = jnp.broadcast_to(ext, (8, width))
    base = roll_rows(wide, 1)
    prev = None
    for q in range(16):
        cur = base if q == 0 else pltpu.roll(base, 8 * q, 1)
        if q % 2 == 0:
            prev = cur
            continue
        pair = jnp.concatenate([prev, cur], axis=0).astype(BF16)
        at = 8 * (q - 1)
        e_ref[at : at + 16, :] = pair[:, BLK:]
        e_ref[128 + at : 128 + at + 16, :] = pair[:, 128 : 128 + length]


def rows_of(ref, half):
    pieces = ref.shape[0]
    part = ref[:, half * CPG : (half + 1) * CPG, :]
    pair = part.reshape(pieces // 2, 2, CPG, 128)
    return jnp.concatenate([pair[:, 0], pair[:, 1]], axis=-1).reshape(pieces // 2 * CPG, BLK)


def put_rows(ref, half, rows):
    pieces = ref.shape[0]
    blocks = rows.reshape(pieces // 2, CPG, BLK)
    both = jnp.stack([blocks[:, :, :128], blocks[:, :, 128:]], axis=1)
    ref[:, half * CPG : (half + 1) * CPG, :] = both.reshape(pieces, CPG, 128)


def conv_kernel(in_ref, e_ref, out_ref, held_ref, x_ref, acc_ref, sem):
    nblocks = in_ref.shape[0] // 2
    x_ref[...] = rows_of(in_ref, 0)
    for d in range(nblocks):
        n = (nblocks - d) * CPG
        part = jnp.dot(
            x_ref[:n, :], e_ref[:, d * BLK : (d + 1) * BLK], preferred_element_type=F32
        )
        if d == 0:
            acc_ref[...] = part
        else:
            acc_ref[d * CPG :, :] += part
    put_rows(held_ref, 0, acc_ref[...].astype(BF16))
    half = pl.ds(0, CPG)
    first = pltpu.make_async_copy(held_ref.at[:, half, :], out_ref.at[:, half, :], sem.at[0])
    first.start()
    x_ref[...] = rows_of(in_ref, 1)
    for d in range(nblocks):
        n = (nblocks - d) * CPG
        part = lax.dot_general(
            x_ref[d * CPG :, :],
            e_ref[:, d * BLK : (d + 1) * BLK],
            (((1,), (1,)), ((), ())),
            preferred_element_type=F32,
        )
        if d == 0:
            acc_ref[...] = part
        else:
            acc_ref[:n, :] += part
    put_rows(held_ref, 1, acc_ref[...].astype(BF16))
    half = pl.ds(CPG, CPG)
    second = pltpu.make_async_copy(held_ref.at[:, half, :], out_ref.at[:, half, :], sem.at[1])
    second.start()
    first.wait()
    second.wait()


def roll_rows(rows, sign):
    width = rows.shape[1]
    row = lax.broadcasted_iota(jnp.int32, rows.shape, 0)
    for bit in (1, 2, 4):
        rows = jnp.where((row & bit) != 0, pltpu.roll(rows, (sign * bit) % width, 1), rows)
    return rows


def lag_kernel(scale, in_ref, out_ref, me_ref, xt_ref, g_ref, s_ref):
    me_ref[...] = jnp.full(me_ref.shape, lax.axis_index("dp"), jnp.int32)
    pieces = in_ref.shape[0]
    total = pieces * CPG
    length = pieces * 128
    xt_ref[...] = in_ref[:, :CPG, :].reshape(total, 128).T
    grads = in_ref[:, CPG:, :].reshape(total, 128)
    g_ref[:total, :128] = grads
    g_ref[: total - CPG, 128:] = grads[CPG:]
    g_ref[total - CPG :, 128:] = jnp.zeros((g_ref.shape[0] - total + CPG, 128), BF16)
    g_ref[total:, :128] = jnp.zeros((g_ref.shape[0] - total, 128), BF16)
    s_ref[:, length:] = jnp.zeros((128, 128), F32)
    for d in range(0, pieces, 2):
        n = -(-(total - d * CPG) // 128) * 128
        s_ref[:, d * 128 : (d + 2) * 128] = jnp.dot(
            xt_ref[:, :n], g_ref[d * CPG : d * CPG + n, :], preferred_element_type=F32
        )
    width = length + 128
    terms = [s_ref[8 * q : 8 * q + 8, :] for q in range(16)]
    shift = 8
    while len(terms) > 1:
        terms = [
            terms[i] + pltpu.roll(terms[i + 1], width - shift, 1) for i in range(0, len(terms), 2)
        ]
        shift *= 2
    sums = jnp.sum(roll_rows(terms[0], -1), axis=0, keepdims=True) * scale
    for i in range(length // 128):
        out_ref[i] = sums[:, 128 * i : 128 * (i + 1)]


def close_kernel(
    in_ref, k_ref, v_ref, q_ref, g_ref, out_ref, gq_ref, gk_ref, gv_ref, held_ref, sem
):
    groups, _, pos = in_ref.shape
    step = groups // PARTS
    span = step * CPG
    copies = []
    for part in range(PARTS):
        at = slice(part * span, (part + 1) * span)
        for h, gates, outs in ((0, (q_ref, g_ref), (out_ref, gq_ref)), (1, (v_ref, k_ref), (gk_ref, gv_ref))):
            rows = in_ref[part * step : (part + 1) * step, h * CPG : (h + 1) * CPG, :]
            wide = rows.reshape(span, pos).T.astype(F32)
            for j in range(2):
                i = 2 * h + j
                held_ref[i, :, at] = (gates[j][:, at].astype(F32) * wide).astype(BF16)
                into = outs[j].at[:, pl.ds(part * span, span)]
                copy = pltpu.make_async_copy(
                    held_ref.at[i, :, pl.ds(part * span, span)], into, sem.at[part, i]
                )
                copy.start()
                copies.append(copy)
    for copy in copies:
        copy.wait()


def halve(terms, me, replicas):
    bit = replicas // 2
    while bit:
        both = terms.reshape(2, bit, 1, 128)
        high = jnp.broadcast_to((me & bit) != 0, (bit, 1, 128))
        kept = jnp.where(high, both[1], both[0])
        away = jnp.where(high, both[0], both[1])
        got = lax.ppermute(away, "dp", [(i, i ^ bit) for i in range(replicas)])
        terms = kept + got
        bit //= 2
    return terms.reshape(1, 128)


def step(query, key_in, value, cotangent, filters):
    seqcount, pos, channels = query.shape
    groups = channels // CPG
    pieces = lax.axis_size("ctx")
    replicas = lax.axis_size("dp")
    length = pos * pieces
    nblocks = length // BLK
    flat = [a.reshape(pos, channels) for a in (key_in, value, query, cotangent)]
    held = jax.ShapeDtypeStruct((groups, 2 * CPG, pos), BF16)
    size = groups * 2 * CPG * pos * 2
    sent, band = call(
        gate_kernel,
        (held, jax.ShapeDtypeStruct((BLK, length), BF16)),
        2 * pos * channels,
        3 * size,
        (VMEM, VMEM),
        in_specs=[ANY] * 5,
        scratch_shapes=[
            pltpu.VMEM((4, pos, channels), BF16),
            pltpu.VMEM((1, length), BF16),
            DMA((PARTS, 4)),
            DMA,
        ],
        name="gate",
    )(*[pltpu.with_memory_space_constraint(a, pltpu.HBM) for a in (*flat, filters)])
    owned = lax.all_to_all(sent, "ctx", split_axis=0, concat_axis=0, tiled=True)
    work = 2 * CPG * length * length
    result = call(
        conv_kernel,
        held,
        2 * work,
        2 * size + BLK * length * 2,
        ANY,
        in_specs=[VMEM] * 2,
        scratch_shapes=[
            pltpu.VMEM(held.shape, BF16),
            pltpu.VMEM((nblocks * CPG, BLK), BF16),
            pltpu.VMEM((nblocks * CPG, BLK), F32),
            DMA((2,)),
        ],
        name="conv",
    )(owned, band)
    owned, result = lax.optimization_barrier((owned, result))
    back = lax.all_to_all(result, "ctx", split_axis=0, concat_axis=0, tiled=True)
    scale = 1.0 / math.sqrt(seqcount * replicas * length * CPG)

    def lag_body(*refs):
        lag_kernel(scale, *refs)

    lags_of = call(
        lag_body,
        (
            jax.ShapeDtypeStruct((length // 128, 1, 128), F32),
            jax.ShapeDtypeStruct((1, 128), jnp.int32),
        ),
        work,
        size + BLK * length * 8,
        (VMEM, VMEM),
        in_specs=[VMEM],
        scratch_shapes=[
            pltpu.VMEM((128, pieces * CPG), BF16),
            pltpu.VMEM((pieces * CPG + 128, 256), BF16),
            pltpu.VMEM((128, length + 128), F32),
        ],
        name="lags",
    )
    lags, me = lags_of(owned)
    grad_filter = halve(lags, me, replicas)
    wide = jax.ShapeDtypeStruct((pos, channels), BF16)
    close = call(
        close_kernel,
        (wide,) * 4,
        4 * pos * channels,
        5 * size,
        (ANY,) * 4,
        in_specs=[VMEM] * 5,
        scratch_shapes=[pltpu.VMEM((4, pos, channels), BF16), DMA((PARTS, 4))],
        name="close",
    )
    outs = close(back, *flat)
    return tuple(o.reshape(seqcount, pos, channels) for o in outs) + (grad_filter,)


def solution(mesh):
    spread = P("dp", "ctx", None)
    return jax.shard_map(
        step,
        mesh=mesh,
        in_specs=(spread,) * 4 + (P("ctx", None),),
        out_specs=(spread,) * 4 + (P("ctx", "dp"),),
        check_vma=False,
    )
```

```python
import math

import jax
import jax.numpy as jnp
from jax import lax
from jax.experimental import pallas as pl
from jax.experimental.pallas import tpu as pltpu
from jax.sharding import PartitionSpec as P


CPG = 32
BLK = 256
VMEM = pl.BlockSpec(memory_space=pltpu.VMEM)
F32 = jnp.float32
BF16 = jnp.bfloat16


ANY = pl.BlockSpec(memory_space=pl.ANY)
DMA = pltpu.SemaphoreType.DMA
PARTS = 4


def call(kernel, out_shape, flops, moved, outs, limit=16, **kw):
    return pl.pallas_call(
        kernel,
        out_shape=out_shape,
        out_specs=outs,
        cost_estimate=pl.CostEstimate(flops=flops, bytes_accessed=moved, transcendentals=0),
        compiler_params=pltpu.CompilerParams(vmem_limit_bytes=limit * 2**20),
        **kw,
    )


def gate_kernel(k_ref, v_ref, q_ref, g_ref, out_ref, wide_ref, in_sem):
    groups, _, pos = out_ref.shape
    step = groups // PARTS
    span = step * CPG
    loads = []
    for part in range(PARTS):
        at = pl.ds(part * span, span)
        row = [
            pltpu.make_async_copy(ref.at[:, at], wide_ref.at[i, :, at], in_sem.at[part, i])
            for i, ref in enumerate((k_ref, v_ref, g_ref, q_ref))
        ]
        for copy in row:
            copy.start()
        loads.append(row)
    for part in range(PARTS):
        for copy in loads[part]:
            copy.wait()
        at = slice(part * span, (part + 1) * span)
        mine = slice(part * step, (part + 1) * step)
        for h in range(2):
            one = wide_ref[2 * h, :, at].astype(F32) * wide_ref[2 * h + 1, :, at].astype(F32)
            rows = one.astype(BF16).T.reshape(step, CPG, pos)
            out_ref[mine, h * CPG : (h + 1) * CPG, :] = rows


def fill_band(taps, e_ref):
    length = taps.shape[1]
    ext = jnp.concatenate([jnp.zeros((1, BLK), F32), taps.astype(F32)], axis=1)
    width = length + BLK
    wide = jnp.broadcast_to(ext, (8, width))
    base = roll_rows(wide, 1)
    prev = None
    for q in range(16):
        cur = base if q == 0 else pltpu.roll(base, 8 * q, 1)
        if q % 2 == 0:
            prev = cur
            continue
        pair = jnp.concatenate([prev, cur], axis=0).astype(BF16)
        at = 8 * (q - 1)
        e_ref[at : at + 16, :] = pair[:, 128:]


def rows_of(ref, half):
    pieces = ref.shape[0]
    part = ref[:, half * CPG : (half + 1) * CPG, :]
    pair = part.reshape(pieces // 2, 2, CPG, 128)
    return jnp.concatenate([pair[:, 0], pair[:, 1]], axis=-1).reshape(pieces // 2 * CPG, BLK)


def put_rows(ref, half, first, rows):
    count = rows.shape[0] // CPG
    blocks = rows.reshape(count, CPG, BLK)
    both = jnp.stack([blocks[:, :, :128], blocks[:, :, 128:]], axis=1)
    into = slice(2 * first, 2 * (first + count))
    ref[into, half * CPG : (half + 1) * CPG, :] = both.reshape(2 * count, CPG, 128)


def conv_kernel(in_ref, f_ref, out_ref, held_ref, e_ref, x_ref, acc_ref, sem):
    fill_band(f_ref[...], e_ref)
    nblocks = in_ref.shape[0] // 2
    copies = []

    def finish(half, first, count):
        rows = acc_ref[first * CPG : (first + count) * CPG, :].astype(BF16)
        put_rows(held_ref, half, first, rows)
        at = (pl.ds(2 * first, 2 * count), pl.ds(half * CPG, CPG), slice(None))
        copy = pltpu.make_async_copy(held_ref.at[at], out_ref.at[at], sem.at[len(copies)])
        copy.start()
        copies.append(copy)

    def block(d):
        at = d * BLK
        return jnp.concatenate(
            [e_ref[:, at + 128 : at + 128 + BLK], e_ref[:, at : at + BLK]], axis=0
        )

    quarter = nblocks // 4
    x_ref[...] = rows_of(in_ref, 0)
    for d in range(nblocks):
        n = (nblocks - d) * CPG
        part = jnp.dot(x_ref[:n, :], block(d), preferred_element_type=F32)
        if d == 0:
            acc_ref[...] = part
        else:
            acc_ref[d * CPG :, :] += part
    finish(0, 0, nblocks)
    x_ref[...] = rows_of(in_ref, 1)
    for d in range(nblocks):
        n = (nblocks - d) * CPG
        part = lax.dot_general(
            x_ref[d * CPG :, :],
            block(d),
            (((1,), (1,)), ((), ())),
            preferred_element_type=F32,
        )
        if d == 0:
            acc_ref[...] = part
        else:
            acc_ref[:n, :] += part
        if (d + 1) % quarter == 0 and d + 1 >= 2 * quarter:
            count = 2 * quarter if d + 1 == 2 * quarter else quarter
            finish(1, nblocks - d - 1, count)
    for copy in copies:
        copy.wait()


def roll_rows(rows, sign):
    width = rows.shape[1]
    row = lax.broadcasted_iota(jnp.int32, rows.shape, 0)
    for bit in (1, 2, 4):
        rows = jnp.where((row & bit) != 0, pltpu.roll(rows, (sign * bit) % width, 1), rows)
    return rows


def lag_kernel(scale, in_ref, out_ref, me_ref, xt_ref, g_ref, s_ref):
    me_ref[...] = jnp.full(me_ref.shape, lax.axis_index("dp"), jnp.int32)
    pieces = in_ref.shape[0]
    total = pieces * CPG
    length = pieces * 128
    xt_ref[...] = in_ref[:, :CPG, :].reshape(total, 128).T
    grads = in_ref[:, CPG:, :].reshape(total, 128)
    g_ref[:total, :128] = grads
    g_ref[: total - CPG, 128:] = grads[CPG:]
    g_ref[total - CPG :, 128:] = jnp.zeros((g_ref.shape[0] - total + CPG, 128), BF16)
    g_ref[total:, :128] = jnp.zeros((g_ref.shape[0] - total, 128), BF16)
    s_ref[:, length:] = jnp.zeros((128, 128), F32)
    for d in range(0, pieces, 2):
        n = -(-(total - d * CPG) // 128) * 128
        s_ref[:, d * 128 : (d + 2) * 128] = jnp.dot(
            xt_ref[:, :n], g_ref[d * CPG : d * CPG + n, :], preferred_element_type=F32
        )
    width = length + 128
    terms = [s_ref[8 * q : 8 * q + 8, :] for q in range(16)]
    shift = 8
    while len(terms) > 1:
        terms = [
            terms[i] + pltpu.roll(terms[i + 1], width - shift, 1) for i in range(0, len(terms), 2)
        ]
        shift *= 2
    sums = jnp.sum(roll_rows(terms[0], -1), axis=0, keepdims=True) * scale
    for i in range(length // 128):
        out_ref[i] = sums[:, 128 * i : 128 * (i + 1)]


def close_kernel(
    in_ref, k_ref, v_ref, q_ref, g_ref, out_ref, gq_ref, gk_ref, gv_ref, held_ref, sem
):
    groups, _, pos = in_ref.shape
    step = groups // PARTS
    span = step * CPG
    copies = []
    for part in range(PARTS):
        at = slice(part * span, (part + 1) * span)
        for h, gates, outs in ((0, (q_ref, g_ref), (out_ref, gq_ref)), (1, (v_ref, k_ref), (gk_ref, gv_ref))):
            rows = in_ref[part * step : (part + 1) * step, h * CPG : (h + 1) * CPG, :]
            wide = rows.reshape(span, pos).T.astype(F32)
            for j in range(2):
                i = 2 * h + j
                held_ref[i, :, at] = (gates[j][:, at].astype(F32) * wide).astype(BF16)
                into = outs[j].at[:, pl.ds(part * span, span)]
                copy = pltpu.make_async_copy(
                    held_ref.at[i, :, pl.ds(part * span, span)], into, sem.at[part, i]
                )
                copy.start()
                copies.append(copy)
    for copy in copies:
        copy.wait()


def halve(terms, me, replicas):
    bit = replicas // 2
    while bit:
        both = terms.reshape(2, bit, 1, 128)
        mask = bit + bit // 2 if bit == replicas // 2 else bit
        high = jnp.broadcast_to((me & bit) != 0, (bit, 1, 128))
        kept = jnp.where(high, both[1], both[0])
        away = jnp.where(high, both[0], both[1])
        got = lax.ppermute(away, "dp", [(i, i ^ mask) for i in range(replicas)])
        terms = kept + got
        bit //= 2
    return terms.reshape(1, 128)


def step(query, key_in, value, cotangent, filters):
    seqcount, pos, channels = query.shape
    groups = channels // CPG
    pieces = lax.axis_size("ctx")
    replicas = lax.axis_size("dp")
    length = pos * pieces
    nblocks = length // BLK
    flat = [a.reshape(pos, channels) for a in (key_in, value, query, cotangent)]
    held = jax.ShapeDtypeStruct((groups, 2 * CPG, pos), BF16)
    size = groups * 2 * CPG * pos * 2
    sent = call(
        gate_kernel,
        held,
        2 * pos * channels,
        3 * size,
        VMEM,
        in_specs=[ANY] * 4,
        scratch_shapes=[pltpu.VMEM((4, pos, channels), BF16), DMA((PARTS, 4))],
        name="gate",
    )(*[pltpu.with_memory_space_constraint(a, pltpu.HBM) for a in flat])
    owned = lax.all_to_all(sent, "ctx", split_axis=0, concat_axis=0, tiled=True)
    work = 2 * CPG * length * length
    result = call(
        conv_kernel,
        held,
        2 * work,
        2 * size + BLK * length * 2,
        ANY,
        in_specs=[VMEM] * 2,
        scratch_shapes=[
            pltpu.VMEM(held.shape, BF16),
            pltpu.VMEM((128, length + 128), BF16),
            pltpu.VMEM((nblocks * CPG, BLK), BF16),
            pltpu.VMEM((nblocks * CPG, BLK), F32),
            DMA((4,)),
        ],
        name="conv",
    )(owned, filters)
    owned, result = lax.optimization_barrier((owned, result))
    back = lax.all_to_all(result, "ctx", split_axis=0, concat_axis=0, tiled=True)
    scale = 1.0 / math.sqrt(seqcount * replicas * length * CPG)

    def lag_body(*refs):
        lag_kernel(scale, *refs)

    lags_of = call(
        lag_body,
        (
            jax.ShapeDtypeStruct((length // 128, 1, 128), F32),
            jax.ShapeDtypeStruct((1, 128), jnp.int32),
        ),
        work,
        size + BLK * length * 8,
        (VMEM, VMEM),
        in_specs=[VMEM],
        scratch_shapes=[
            pltpu.VMEM((128, pieces * CPG), BF16),
            pltpu.VMEM((pieces * CPG + 128, 256), BF16),
            pltpu.VMEM((128, length + 128), F32),
        ],
        name="lags",
    )
    lags, me = lags_of(owned)
    grad_filter = halve(lags, me, replicas)
    wide = jax.ShapeDtypeStruct((pos, channels), BF16)
    close = call(
        close_kernel,
        (wide,) * 4,
        4 * pos * channels,
        5 * size,
        (ANY,) * 4,
        in_specs=[VMEM] * 5,
        scratch_shapes=[pltpu.VMEM((4, pos, channels), BF16), DMA((PARTS, 4))],
        name="close",
    )
    outs = close(back, *flat)
    return tuple(o.reshape(seqcount, pos, channels) for o in outs) + (grad_filter,)


def solution(mesh):
    spread = P("dp", "ctx", None)
    return jax.shard_map(
        step,
        mesh=mesh,
        in_specs=(spread,) * 4 + (P("ctx", None),),
        out_specs=(spread,) * 4 + (P("ctx", "dp"),),
        check_vma=False,
    )
```

```python
import math

import jax
import jax.numpy as jnp
from jax import lax
from jax.experimental import pallas as pl
from jax.experimental.pallas import tpu as pltpu
from jax.sharding import PartitionSpec as P


CPG = 32
BLK = 256
VMEM = pl.BlockSpec(memory_space=pltpu.VMEM)
F32 = jnp.float32
BF16 = jnp.bfloat16


ANY = pl.BlockSpec(memory_space=pl.ANY)
DMA = pltpu.SemaphoreType.DMA
PARTS = 4


def call(kernel, out_shape, flops, moved, outs, limit=16, **kw):
    return pl.pallas_call(
        kernel,
        out_shape=out_shape,
        out_specs=outs,
        cost_estimate=pl.CostEstimate(flops=flops, bytes_accessed=moved, transcendentals=0),
        compiler_params=pltpu.CompilerParams(vmem_limit_bytes=limit * 2**20),
        **kw,
    )


def gate_kernel(k_ref, v_ref, q_ref, g_ref, out_ref, wide_ref, in_sem):
    groups, _, pos = out_ref.shape
    step = groups // PARTS
    span = step * CPG
    loads = []
    for part in range(PARTS):
        at = pl.ds(part * span, span)
        row = [
            pltpu.make_async_copy(ref.at[:, at], wide_ref.at[i, :, at], in_sem.at[part, i])
            for i, ref in enumerate((k_ref, v_ref, g_ref, q_ref))
        ]
        for copy in row:
            copy.start()
        loads.append(row)
    for part in range(PARTS):
        for copy in loads[part]:
            copy.wait()
        at = slice(part * span, (part + 1) * span)
        mine = slice(part * step, (part + 1) * step)
        for h in range(2):
            one = wide_ref[2 * h, :, at].astype(F32) * wide_ref[2 * h + 1, :, at].astype(F32)
            rows = one.astype(BF16).T.reshape(step, CPG, pos)
            out_ref[mine, h * CPG : (h + 1) * CPG, :] = rows


def fill_band(taps, e_ref):
    length = taps.shape[1]
    ext = jnp.concatenate([jnp.zeros((1, BLK), F32), taps.astype(F32)], axis=1)
    width = length + BLK
    wide = jnp.broadcast_to(ext, (8, width))
    base = roll_rows(wide, 1)
    prev = None
    for q in range(16):
        cur = base if q == 0 else pltpu.roll(base, 8 * q, 1)
        if q % 2 == 0:
            prev = cur
            continue
        pair = jnp.concatenate([prev, cur], axis=0).astype(BF16)
        at = 8 * (q - 1)
        e_ref[at : at + 16, :] = pair[:, BLK:]
        e_ref[128 + at : 128 + at + 16, :] = pair[:, 128 : 128 + length]


def rows_of(ref, half):
    pieces = ref.shape[0]
    part = ref[:, half * CPG : (half + 1) * CPG, :]
    pair = part.reshape(pieces // 2, 2, CPG, 128)
    return jnp.concatenate([pair[:, 0], pair[:, 1]], axis=-1).reshape(pieces // 2 * CPG, BLK)


def put_rows(ref, half, rows):
    pieces = ref.shape[0]
    blocks = rows.reshape(pieces // 2, CPG, BLK)
    both = jnp.stack([blocks[:, :, :128], blocks[:, :, 128:]], axis=1)
    ref[:, half * CPG : (half + 1) * CPG, :] = both.reshape(pieces, CPG, 128)


def conv_kernel(in_ref, f_ref, out_ref, held_ref, e_ref, x_ref, acc_ref, sem):
    fill_band(f_ref[...], e_ref)
    nblocks = in_ref.shape[0] // 2
    x_ref[...] = rows_of(in_ref, 0)
    for d in range(nblocks):
        n = (nblocks - d) * CPG
        part = jnp.dot(
            x_ref[:n, :], e_ref[:, d * BLK : (d + 1) * BLK], preferred_element_type=F32
        )
        if d == 0:
            acc_ref[...] = part
        else:
            acc_ref[d * CPG :, :] += part
    put_rows(held_ref, 0, acc_ref[...].astype(BF16))
    half = pl.ds(0, CPG)
    first = pltpu.make_async_copy(held_ref.at[:, half, :], out_ref.at[:, half, :], sem.at[0])
    first.start()
    x_ref[...] = rows_of(in_ref, 1)
    for d in range(nblocks):
        n = (nblocks - d) * CPG
        part = lax.dot_general(
            x_ref[d * CPG :, :],
            e_ref[:, d * BLK : (d + 1) * BLK],
            (((1,), (1,)), ((), ())),
            preferred_element_type=F32,
        )
        if d == 0:
            acc_ref[...] = part
        else:
            acc_ref[:n, :] += part
    put_rows(held_ref, 1, acc_ref[...].astype(BF16))
    half = pl.ds(CPG, CPG)
    second = pltpu.make_async_copy(held_ref.at[:, half, :], out_ref.at[:, half, :], sem.at[1])
    second.start()
    first.wait()
    second.wait()


def roll_rows(rows, sign):
    width = rows.shape[1]
    row = lax.broadcasted_iota(jnp.int32, rows.shape, 0)
    for bit in (1, 2, 4):
        rows = jnp.where((row & bit) != 0, pltpu.roll(rows, (sign * bit) % width, 1), rows)
    return rows


def lag_kernel(scale, in_ref, out_ref, me_ref, xt_ref, g_ref, s_ref):
    me_ref[...] = jnp.full(me_ref.shape, lax.axis_index("dp"), jnp.int32)
    pieces = in_ref.shape[0]
    total = pieces * CPG
    length = pieces * 128
    xt_ref[...] = in_ref[:, :CPG, :].reshape(total, 128).T
    grads = in_ref[:, CPG:, :].reshape(total, 128)
    g_ref[:total, :128] = grads
    g_ref[: total - CPG, 128:] = grads[CPG:]
    g_ref[total - CPG :, 128:] = jnp.zeros((g_ref.shape[0] - total + CPG, 128), BF16)
    g_ref[total:, :128] = jnp.zeros((g_ref.shape[0] - total, 128), BF16)
    s_ref[:, length:] = jnp.zeros((128, 128), F32)
    for d in range(0, pieces, 2):
        n = -(-(total - d * CPG) // 128) * 128
        s_ref[:, d * 128 : (d + 2) * 128] = jnp.dot(
            xt_ref[:, :n], g_ref[d * CPG : d * CPG + n, :], preferred_element_type=F32
        )
    width = length + 128
    terms = [s_ref[8 * q : 8 * q + 8, :] for q in range(16)]
    shift = 8
    while len(terms) > 1:
        terms = [
            terms[i] + pltpu.roll(terms[i + 1], width - shift, 1) for i in range(0, len(terms), 2)
        ]
        shift *= 2
    sums = jnp.sum(roll_rows(terms[0], -1), axis=0, keepdims=True) * scale
    for i in range(length // 128):
        out_ref[i] = sums[:, 128 * i : 128 * (i + 1)]


def close_kernel(
    in_ref,
    k_ref,
    v_ref,
    q_ref,
    g_ref,
    kept_ref,
    got_ref,
    out_ref,
    gq_ref,
    gk_ref,
    gv_ref,
    gf_ref,
    held_ref,
    sum_ref,
    sem,
    sum_sem,
):
    sum_ref[...] = kept_ref[0] + got_ref[0]
    sums = pltpu.make_async_copy(sum_ref, gf_ref, sum_sem)
    groups, _, pos = in_ref.shape
    step = groups // PARTS
    span = step * CPG
    copies = []
    for part in range(PARTS):
        if part == 1:
            sums.start()
        at = slice(part * span, (part + 1) * span)
        for h, gates, outs in ((0, (q_ref, g_ref), (out_ref, gq_ref)), (1, (v_ref, k_ref), (gk_ref, gv_ref))):
            rows = in_ref[part * step : (part + 1) * step, h * CPG : (h + 1) * CPG, :]
            wide = rows.reshape(span, pos).T.astype(F32)
            for j in range(2):
                i = 2 * h + j
                held_ref[i, :, at] = (gates[j][:, at].astype(F32) * wide).astype(BF16)
                into = outs[j].at[:, pl.ds(part * span, span)]
                copy = pltpu.make_async_copy(
                    held_ref.at[i, :, pl.ds(part * span, span)], into, sem.at[part, i]
                )
                copy.start()
                copies.append(copy)
    for copy in copies:
        copy.wait()
    sums.wait()


def halve(terms, me, replicas):
    bit = replicas // 2
    while bit:
        both = terms.reshape(2, bit, 1, 128)
        mask = bit + bit // 2 if bit == replicas // 2 else bit
        high = jnp.broadcast_to((me & bit) != 0, (bit, 1, 128))
        kept = jnp.where(high, both[1], both[0])
        away = jnp.where(high, both[0], both[1])
        got = lax.ppermute(away, "dp", [(i, i ^ mask) for i in range(replicas)])
        terms = kept + got
        bit //= 2
    return kept, got


def step(query, key_in, value, cotangent, filters):
    seqcount, pos, channels = query.shape
    groups = channels // CPG
    pieces = lax.axis_size("ctx")
    replicas = lax.axis_size("dp")
    length = pos * pieces
    nblocks = length // BLK
    flat = [a.reshape(pos, channels) for a in (key_in, value, query, cotangent)]
    held = jax.ShapeDtypeStruct((groups, 2 * CPG, pos), BF16)
    size = groups * 2 * CPG * pos * 2
    sent = call(
        gate_kernel,
        held,
        2 * pos * channels,
        3 * size,
        VMEM,
        in_specs=[ANY] * 4,
        scratch_shapes=[pltpu.VMEM((4, pos, channels), BF16), DMA((PARTS, 4))],
        name="gate",
    )(*[pltpu.with_memory_space_constraint(a, pltpu.HBM) for a in flat])
    owned = lax.all_to_all(sent, "ctx", split_axis=0, concat_axis=0, tiled=True)
    work = 2 * CPG * length * length
    result = call(
        conv_kernel,
        held,
        2 * work,
        2 * size + BLK * length * 2,
        ANY,
        in_specs=[VMEM] * 2,
        scratch_shapes=[
            pltpu.VMEM(held.shape, BF16),
            pltpu.VMEM((BLK, length), BF16),
            pltpu.VMEM((nblocks * CPG, BLK), BF16),
            pltpu.VMEM((nblocks * CPG, BLK), F32),
            DMA((2,)),
        ],
        name="conv",
    )(owned, filters)
    owned, result = lax.optimization_barrier((owned, result))
    back = lax.all_to_all(result, "ctx", split_axis=0, concat_axis=0, tiled=True)
    scale = 1.0 / math.sqrt(seqcount * replicas * length * CPG)

    def lag_body(*refs):
        lag_kernel(scale, *refs)

    lags_of = call(
        lag_body,
        (
            jax.ShapeDtypeStruct((length // 128, 1, 128), F32),
            jax.ShapeDtypeStruct((1, 128), jnp.int32),
        ),
        work,
        size + BLK * length * 8,
        (VMEM, VMEM),
        in_specs=[VMEM],
        scratch_shapes=[
            pltpu.VMEM((128, pieces * CPG), BF16),
            pltpu.VMEM((pieces * CPG + 128, 256), BF16),
            pltpu.VMEM((128, length + 128), F32),
        ],
        name="lags",
    )
    lags, me = lags_of(owned)
    last = halve(lags, me, replicas)
    wide = jax.ShapeDtypeStruct((pos, channels), BF16)
    close = call(
        close_kernel,
        (wide,) * 4 + (jax.ShapeDtypeStruct((1, 128), F32),),
        4 * pos * channels,
        5 * size,
        (ANY,) * 5,
        in_specs=[VMEM] * 7,
        scratch_shapes=[
            pltpu.VMEM((4, pos, channels), BF16),
            pltpu.VMEM((1, 128), F32),
            DMA((PARTS, 4)),
            DMA,
        ],
        name="close",
    )
    *outs, grad_filter = close(back, *flat, *last)
    return tuple(o.reshape(seqcount, pos, channels) for o in outs) + (grad_filter,)


def solution(mesh):
    spread = P("dp", "ctx", None)
    return jax.shard_map(
        step,
        mesh=mesh,
        in_specs=(spread,) * 4 + (P("ctx", None),),
        out_specs=(spread,) * 4 + (P("ctx", "dp"),),
        check_vma=False,
    )
```

```python
import math

import jax
import jax.numpy as jnp
from jax import lax
from jax.experimental import pallas as pl
from jax.experimental.pallas import tpu as pltpu
from jax.sharding import PartitionSpec as P


CPG = 32
BLK = 256
VMEM = pl.BlockSpec(memory_space=pltpu.VMEM)
F32 = jnp.float32
BF16 = jnp.bfloat16


ANY = pl.BlockSpec(memory_space=pl.ANY)
DMA = pltpu.SemaphoreType.DMA
PARTS = 4


def call(kernel, out_shape, flops, moved, outs, limit=16, **kw):
    return pl.pallas_call(
        kernel,
        out_shape=out_shape,
        out_specs=outs,
        cost_estimate=pl.CostEstimate(flops=flops, bytes_accessed=moved, transcendentals=0),
        compiler_params=pltpu.CompilerParams(vmem_limit_bytes=limit * 2**20),
        **kw,
    )


def gate_kernel(k_ref, v_ref, q_ref, g_ref, out_ref, wide_ref, in_sem):
    groups, _, pos = out_ref.shape
    step = groups // PARTS
    span = step * CPG
    loads = []
    for part in range(PARTS):
        at = pl.ds(part * span, span)
        row = [
            pltpu.make_async_copy(ref.at[:, at], wide_ref.at[i, :, at], in_sem.at[part, i])
            for i, ref in enumerate((k_ref, v_ref, g_ref, q_ref))
        ]
        for copy in row:
            copy.start()
        loads.append(row)
    for part in range(PARTS):
        for copy in loads[part]:
            copy.wait()
        at = slice(part * span, (part + 1) * span)
        mine = slice(part * step, (part + 1) * step)
        for h in range(2):
            one = wide_ref[2 * h, :, at].astype(F32) * wide_ref[2 * h + 1, :, at].astype(F32)
            rows = one.astype(BF16).T.reshape(step, CPG, pos)
            out_ref[mine, h * CPG : (h + 1) * CPG, :] = rows


def fill_band(taps, e_ref):
    length = taps.shape[1]
    ext = jnp.concatenate([jnp.zeros((1, BLK), F32), taps.astype(F32)], axis=1)
    width = length + BLK
    wide = jnp.broadcast_to(ext, (8, width))
    row = lax.broadcasted_iota(jnp.int32, (8, width), 0)
    base = wide
    for r in range(1, 8):
        base = jnp.where(row == r, pltpu.roll(wide, r, 1), base)
    prev = None
    for q in range(16):
        cur = base if q == 0 else pltpu.roll(base, 8 * q, 1)
        if q % 2 == 0:
            prev = cur
            continue
        pair = jnp.concatenate([prev, cur], axis=0).astype(BF16)
        at = 8 * (q - 1)
        e_ref[at : at + 16, :] = pair[:, BLK:]
        e_ref[128 + at : 128 + at + 16, :] = pair[:, 128 : 128 + length]


def rows_of(ref, half):
    pieces = ref.shape[0]
    part = ref[:, half * CPG : (half + 1) * CPG, :]
    pair = part.reshape(pieces // 2, 2, CPG, 128)
    return jnp.concatenate([pair[:, 0], pair[:, 1]], axis=-1).reshape(pieces // 2 * CPG, BLK)


def put_rows(ref, half, rows):
    pieces = ref.shape[0]
    blocks = rows.reshape(pieces // 2, CPG, BLK)
    both = jnp.stack([blocks[:, :, :128], blocks[:, :, 128:]], axis=1)
    ref[:, half * CPG : (half + 1) * CPG, :] = both.reshape(pieces, CPG, 128)


def conv_kernel(in_ref, f_ref, out_ref, held_ref, e_ref, x_ref, acc_ref, sem):
    fill_band(f_ref[...], e_ref)
    nblocks = in_ref.shape[0] // 2
    x_ref[...] = rows_of(in_ref, 0)
    for d in range(nblocks):
        n = (nblocks - d) * CPG
        part = jnp.dot(
            x_ref[:n, :], e_ref[:, d * BLK : (d + 1) * BLK], preferred_element_type=F32
        )
        if d == 0:
            acc_ref[...] = part
        else:
            acc_ref[d * CPG :, :] += part
    put_rows(held_ref, 0, acc_ref[...].astype(BF16))
    half = pl.ds(0, CPG)
    first = pltpu.make_async_copy(held_ref.at[:, half, :], out_ref.at[:, half, :], sem.at[0])
    first.start()
    x_ref[...] = rows_of(in_ref, 1)
    for d in range(nblocks):
        n = (nblocks - d) * CPG
        part = lax.dot_general(
            x_ref[d * CPG :, :],
            e_ref[:, d * BLK : (d + 1) * BLK],
            (((1,), (1,)), ((), ())),
            preferred_element_type=F32,
        )
        if d == 0:
            acc_ref[...] = part
        else:
            acc_ref[:n, :] += part
    put_rows(held_ref, 1, acc_ref[...].astype(BF16))
    half = pl.ds(CPG, CPG)
    second = pltpu.make_async_copy(held_ref.at[:, half, :], out_ref.at[:, half, :], sem.at[1])
    second.start()
    first.wait()
    second.wait()


def roll_rows(rows):
    width = rows.shape[1]
    row = lax.broadcasted_iota(jnp.int32, rows.shape, 0)
    for bit in (1, 2, 4):
        rows = jnp.where((row & bit) != 0, pltpu.roll(rows, width - bit, 1), rows)
    return rows


def lag_kernel(scale, in_ref, out_ref, me_ref, xt_ref, g_ref, s_ref):
    me_ref[...] = jnp.full(me_ref.shape, lax.axis_index("dp"), jnp.int32)
    pieces = in_ref.shape[0]
    total = pieces * CPG
    length = pieces * 128
    xt_ref[...] = in_ref[:, :CPG, :].reshape(total, 128).T
    grads = in_ref[:, CPG:, :].reshape(total, 128)
    g_ref[:total, :128] = grads
    g_ref[: total - CPG, 128:] = grads[CPG:]
    g_ref[total - CPG :, 128:] = jnp.zeros((g_ref.shape[0] - total + CPG, 128), BF16)
    g_ref[total:, :128] = jnp.zeros((g_ref.shape[0] - total, 128), BF16)
    s_ref[:, length:] = jnp.zeros((128, 128), F32)
    for d in range(0, pieces, 2):
        n = -(-(total - d * CPG) // 128) * 128
        s_ref[:, d * 128 : (d + 2) * 128] = jnp.dot(
            xt_ref[:, :n], g_ref[d * CPG : d * CPG + n, :], preferred_element_type=F32
        )
    width = length + 128
    terms = [s_ref[8 * q : 8 * q + 8, :] for q in range(16)]
    shift = 8
    while len(terms) > 1:
        terms = [
            terms[i] + pltpu.roll(terms[i + 1], width - shift, 1) for i in range(0, len(terms), 2)
        ]
        shift *= 2
    sums = jnp.sum(roll_rows(terms[0]), axis=0, keepdims=True) * scale
    for i in range(length // 128):
        out_ref[i] = sums[:, 128 * i : 128 * (i + 1)]


def close_kernel(
    in_ref,
    k_ref,
    v_ref,
    q_ref,
    g_ref,
    kept_ref,
    got_ref,
    out_ref,
    gq_ref,
    gk_ref,
    gv_ref,
    gf_ref,
    held_ref,
    sum_ref,
    sem,
    sum_sem,
):
    sum_ref[...] = kept_ref[0] + got_ref[0]
    sums = pltpu.make_async_copy(sum_ref, gf_ref, sum_sem)
    groups, _, pos = in_ref.shape
    step = groups // PARTS
    span = step * CPG
    copies = []
    for part in range(PARTS):
        if part == 1:
            sums.start()
        at = slice(part * span, (part + 1) * span)
        for h, gates, outs in ((0, (q_ref, g_ref), (out_ref, gq_ref)), (1, (v_ref, k_ref), (gk_ref, gv_ref))):
            rows = in_ref[part * step : (part + 1) * step, h * CPG : (h + 1) * CPG, :]
            wide = rows.reshape(span, pos).T.astype(F32)
            for j in range(2):
                i = 2 * h + j
                held_ref[i, :, at] = (gates[j][:, at].astype(F32) * wide).astype(BF16)
                into = outs[j].at[:, pl.ds(part * span, span)]
                copy = pltpu.make_async_copy(
                    held_ref.at[i, :, pl.ds(part * span, span)], into, sem.at[part, i]
                )
                copy.start()
                copies.append(copy)
    for copy in copies:
        copy.wait()
    sums.wait()


def halve(terms, me, replicas):
    bit = replicas // 2
    while bit:
        both = terms.reshape(2, bit, 1, 128)
        mask = bit + bit // 2 if bit == replicas // 2 else bit
        high = jnp.broadcast_to((me & bit) != 0, (bit, 1, 128))
        kept = jnp.where(high, both[1], both[0])
        away = jnp.where(high, both[0], both[1])
        got = lax.ppermute(away, "dp", [(i, i ^ mask) for i in range(replicas)])
        terms = kept + got
        bit //= 2
    return kept, got


def step(query, key_in, value, cotangent, filters):
    seqcount, pos, channels = query.shape
    groups = channels // CPG
    pieces = lax.axis_size("ctx")
    replicas = lax.axis_size("dp")
    length = pos * pieces
    nblocks = length // BLK
    flat = [a.reshape(pos, channels) for a in (key_in, value, query, cotangent)]
    held = jax.ShapeDtypeStruct((groups, 2 * CPG, pos), BF16)
    size = groups * 2 * CPG * pos * 2
    sent = call(
        gate_kernel,
        held,
        2 * pos * channels,
        3 * size,
        VMEM,
        in_specs=[ANY] * 4,
        scratch_shapes=[pltpu.VMEM((4, pos, channels), BF16), DMA((PARTS, 4))],
        name="gate",
    )(*[pltpu.with_memory_space_constraint(a, pltpu.HBM) for a in flat])
    owned = lax.all_to_all(sent, "ctx", split_axis=0, concat_axis=0, tiled=True)
    work = 2 * CPG * length * length
    result = call(
        conv_kernel,
        held,
        2 * work,
        2 * size + BLK * length * 2,
        ANY,
        in_specs=[VMEM] * 2,
        scratch_shapes=[
            pltpu.VMEM(held.shape, BF16),
            pltpu.VMEM((BLK, length), BF16),
            pltpu.VMEM((nblocks * CPG, BLK), BF16),
            pltpu.VMEM((nblocks * CPG, BLK), F32),
            DMA((2,)),
        ],
        name="conv",
    )(owned, filters)
    owned, result = lax.optimization_barrier((owned, result))
    back = lax.all_to_all(result, "ctx", split_axis=0, concat_axis=0, tiled=True)
    scale = 1.0 / math.sqrt(seqcount * replicas * length * CPG)

    def lag_body(*refs):
        lag_kernel(scale, *refs)

    lags_of = call(
        lag_body,
        (
            jax.ShapeDtypeStruct((length // 128, 1, 128), F32),
            jax.ShapeDtypeStruct((1, 128), jnp.int32),
        ),
        work,
        size + BLK * length * 8,
        (VMEM, VMEM),
        in_specs=[VMEM],
        scratch_shapes=[
            pltpu.VMEM((128, pieces * CPG), BF16),
            pltpu.VMEM((pieces * CPG + 128, 256), BF16),
            pltpu.VMEM((128, length + 128), F32),
        ],
        name="lags",
    )
    lags, me = lags_of(owned)
    last = halve(lags, me, replicas)
    wide = jax.ShapeDtypeStruct((pos, channels), BF16)
    close = call(
        close_kernel,
        (wide,) * 4 + (jax.ShapeDtypeStruct((1, 128), F32),),
        4 * pos * channels,
        5 * size,
        (ANY,) * 5,
        in_specs=[VMEM] * 7,
        scratch_shapes=[
            pltpu.VMEM((4, pos, channels), BF16),
            pltpu.VMEM((1, 128), F32),
            DMA((PARTS, 4)),
            DMA,
        ],
        name="close",
    )
    *outs, grad_filter = close(back, *flat, *last)
    return tuple(o.reshape(seqcount, pos, channels) for o in outs) + (grad_filter,)


def solution(mesh):
    spread = P("dp", "ctx", None)
    return jax.shard_map(
        step,
        mesh=mesh,
        in_specs=(spread,) * 4 + (P("ctx", None),),
        out_specs=(spread,) * 4 + (P("ctx", "dp"),),
        check_vma=False,
    )
```

```python
import math

import jax
import jax.numpy as jnp
from jax import lax
from jax.experimental import pallas as pl
from jax.experimental.pallas import tpu as pltpu
from jax.sharding import PartitionSpec as P


CPG = 32
BLK = 256
VMEM = pl.BlockSpec(memory_space=pltpu.VMEM)
F32 = jnp.float32
BF16 = jnp.bfloat16


ANY = pl.BlockSpec(memory_space=pl.ANY)
DMA = pltpu.SemaphoreType.DMA
PARTS = 4
LOADS = 2


def call(kernel, out_shape, flops, moved, outs, limit=16, **kw):
    return pl.pallas_call(
        kernel,
        out_shape=out_shape,
        out_specs=outs,
        cost_estimate=pl.CostEstimate(flops=flops, bytes_accessed=moved, transcendentals=0),
        compiler_params=pltpu.CompilerParams(vmem_limit_bytes=limit * 2**20),
        **kw,
    )


def gate_kernel(k_ref, v_ref, q_ref, g_ref, out_ref, wide_ref, in_sem):
    groups, _, pos = out_ref.shape
    step = groups // LOADS
    span = step * CPG
    loads = []
    for part in range(LOADS):
        at = pl.ds(part * span, span)
        row = [
            pltpu.make_async_copy(ref.at[:, at], wide_ref.at[i, :, at], in_sem.at[part, i])
            for i, ref in enumerate((k_ref, v_ref, g_ref, q_ref))
        ]
        for copy in row:
            copy.start()
        loads.append(row)
    for part in range(LOADS):
        for copy in loads[part]:
            copy.wait()
        at = slice(part * span, (part + 1) * span)
        mine = slice(part * step, (part + 1) * step)
        for h in range(2):
            one = wide_ref[2 * h, :, at] * wide_ref[2 * h + 1, :, at]
            rows = one.T.reshape(step, CPG, pos)
            out_ref[mine, h * CPG : (h + 1) * CPG, :] = rows


def fill_band(taps, e_ref):
    length = taps.shape[1]
    ext = jnp.concatenate([jnp.zeros((1, BLK), F32), taps.astype(F32)], axis=1)
    width = length + BLK
    wide = jnp.broadcast_to(ext, (8, width))
    row = lax.broadcasted_iota(jnp.int32, (8, width), 0)
    base = wide
    for r in range(1, 8):
        base = jnp.where(row == r, pltpu.roll(wide, r, 1), base)
    prev = None
    for q in range(16):
        cur = base if q == 0 else pltpu.roll(base, 8 * q, 1)
        if q % 2 == 0:
            prev = cur
            continue
        pair = jnp.concatenate([prev, cur], axis=0).astype(BF16)
        at = 8 * (q - 1)
        e_ref[at : at + 16, :] = pair[:, BLK:]
        e_ref[128 + at : 128 + at + 16, :] = pair[:, 128 : 128 + length]


def rows_of(ref, half):
    pieces = ref.shape[0]
    part = ref[:, half * CPG : (half + 1) * CPG, :]
    pair = part.reshape(pieces // 2, 2, CPG, 128)
    return jnp.concatenate([pair[:, 0], pair[:, 1]], axis=-1).reshape(pieces // 2 * CPG, BLK)


def put_rows(ref, half, rows):
    pieces = ref.shape[0]
    blocks = rows.reshape(pieces // 2, CPG, BLK)
    both = jnp.stack([blocks[:, :, :128], blocks[:, :, 128:]], axis=1)
    ref[:, half * CPG : (half + 1) * CPG, :] = both.reshape(pieces, CPG, 128)


def conv_kernel(in_ref, f_ref, out_ref, held_ref, e_ref, x_ref, acc_ref, sem):
    fill_band(f_ref[...], e_ref)
    nblocks = in_ref.shape[0] // 2
    x_ref[...] = rows_of(in_ref, 0)
    for d in range(nblocks):
        n = (nblocks - d) * CPG
        part = jnp.dot(
            x_ref[:n, :], e_ref[:, d * BLK : (d + 1) * BLK], preferred_element_type=F32
        )
        if d == 0:
            acc_ref[...] = part
        else:
            acc_ref[d * CPG :, :] += part
    put_rows(held_ref, 0, acc_ref[...].astype(BF16))
    half = pl.ds(0, CPG)
    first = pltpu.make_async_copy(held_ref.at[:, half, :], out_ref.at[:, half, :], sem.at[0])
    first.start()
    x_ref[...] = rows_of(in_ref, 1)
    for d in range(nblocks):
        n = (nblocks - d) * CPG
        part = lax.dot_general(
            x_ref[d * CPG :, :],
            e_ref[:, d * BLK : (d + 1) * BLK],
            (((1,), (1,)), ((), ())),
            preferred_element_type=F32,
        )
        if d == 0:
            acc_ref[...] = part
        else:
            acc_ref[:n, :] += part
    put_rows(held_ref, 1, acc_ref[...].astype(BF16))
    half = pl.ds(CPG, CPG)
    second = pltpu.make_async_copy(held_ref.at[:, half, :], out_ref.at[:, half, :], sem.at[1])
    second.start()
    first.wait()
    second.wait()


def roll_rows(rows):
    width = rows.shape[1]
    row = lax.broadcasted_iota(jnp.int32, rows.shape, 0)
    for bit in (1, 2, 4):
        rows = jnp.where((row & bit) != 0, pltpu.roll(rows, width - bit, 1), rows)
    return rows


def lag_kernel(scale, in_ref, out_ref, me_ref, xt_ref, g_ref, s_ref):
    me_ref[...] = jnp.full(me_ref.shape, lax.axis_index("dp"), jnp.int32)
    pieces = in_ref.shape[0]
    total = pieces * CPG
    length = pieces * 128
    xt_ref[...] = in_ref[:, :CPG, :].reshape(total, 128).T
    grads = in_ref[:, CPG:, :].reshape(total, 128)
    g_ref[:total, :128] = grads
    g_ref[: total - CPG, 128:] = grads[CPG:]
    g_ref[total - CPG :, 128:] = jnp.zeros((g_ref.shape[0] - total + CPG, 128), BF16)
    g_ref[total:, :128] = jnp.zeros((g_ref.shape[0] - total, 128), BF16)
    s_ref[:, length:] = jnp.zeros((128, 128), F32)
    for d in range(0, pieces, 2):
        n = -(-(total - d * CPG) // 128) * 128
        s_ref[:, d * 128 : (d + 2) * 128] = jnp.dot(
            xt_ref[:, :n], g_ref[d * CPG : d * CPG + n, :], preferred_element_type=F32
        )
    width = length + 128
    terms = [s_ref[8 * q : 8 * q + 8, :] for q in range(16)]
    shift = 8
    while len(terms) > 1:
        terms = [
            terms[i] + pltpu.roll(terms[i + 1], width - shift, 1) for i in range(0, len(terms), 2)
        ]
        shift *= 2
    sums = jnp.sum(roll_rows(terms[0]), axis=0, keepdims=True) * scale
    for i in range(length // 128):
        out_ref[i] = sums[:, 128 * i : 128 * (i + 1)]


def close_kernel(
    in_ref,
    k_ref,
    v_ref,
    q_ref,
    g_ref,
    kept_ref,
    got_ref,
    out_ref,
    gq_ref,
    gk_ref,
    gv_ref,
    gf_ref,
    held_ref,
    sum_ref,
    sem,
    sum_sem,
):
    sum_ref[...] = kept_ref[0] + got_ref[0]
    sums = pltpu.make_async_copy(sum_ref, gf_ref, sum_sem)
    groups, _, pos = in_ref.shape
    step = groups // PARTS
    span = step * CPG
    copies = []
    for part in range(PARTS):
        if part == 1:
            sums.start()
        at = slice(part * span, (part + 1) * span)
        for h, gates, outs in ((0, (q_ref, g_ref), (out_ref, gq_ref)), (1, (v_ref, k_ref), (gk_ref, gv_ref))):
            rows = in_ref[part * step : (part + 1) * step, h * CPG : (h + 1) * CPG, :]
            wide = rows.reshape(span, pos).T
            for j in range(2):
                i = 2 * h + j
                held_ref[i, :, at] = gates[j][:, at] * wide
                into = outs[j].at[:, pl.ds(part * span, span)]
                copy = pltpu.make_async_copy(
                    held_ref.at[i, :, pl.ds(part * span, span)], into, sem.at[part, i]
                )
                copy.start()
                copies.append(copy)
    for copy in copies:
        copy.wait()
    sums.wait()


def halve(terms, me, replicas):
    bit = replicas // 2
    while bit:
        both = terms.reshape(2, bit, 1, 128)
        mask = bit + bit // 2 if bit == replicas // 2 else bit
        high = jnp.broadcast_to((me & bit) != 0, (bit, 1, 128))
        kept = jnp.where(high, both[1], both[0])
        away = jnp.where(high, both[0], both[1])
        got = lax.ppermute(away, "dp", [(i, i ^ mask) for i in range(replicas)])
        terms = kept + got
        bit //= 2
    return kept, got


def step(query, key_in, value, cotangent, filters):
    seqcount, pos, channels = query.shape
    groups = channels // CPG
    pieces = lax.axis_size("ctx")
    replicas = lax.axis_size("dp")
    length = pos * pieces
    nblocks = length // BLK
    flat = [a.reshape(pos, channels) for a in (key_in, value, query, cotangent)]
    held = jax.ShapeDtypeStruct((groups, 2 * CPG, pos), BF16)
    size = groups * 2 * CPG * pos * 2
    sent = call(
        gate_kernel,
        held,
        2 * pos * channels,
        3 * size,
        VMEM,
        in_specs=[ANY] * 4,
        scratch_shapes=[pltpu.VMEM((4, pos, channels), BF16), DMA((LOADS, 4))],
        name="gate",
    )(*[pltpu.with_memory_space_constraint(a, pltpu.HBM) for a in flat])
    owned = lax.all_to_all(sent, "ctx", split_axis=0, concat_axis=0, tiled=True)
    work = 2 * CPG * length * length
    result = call(
        conv_kernel,
        held,
        2 * work,
        2 * size + BLK * length * 2,
        ANY,
        in_specs=[VMEM] * 2,
        scratch_shapes=[
            pltpu.VMEM(held.shape, BF16),
            pltpu.VMEM((BLK, length), BF16),
            pltpu.VMEM((nblocks * CPG, BLK), BF16),
            pltpu.VMEM((nblocks * CPG, BLK), F32),
            DMA((2,)),
        ],
        name="conv",
    )(owned, filters)
    owned, result = lax.optimization_barrier((owned, result))
    back = lax.all_to_all(result, "ctx", split_axis=0, concat_axis=0, tiled=True)
    scale = 1.0 / math.sqrt(seqcount * replicas * length * CPG)

    def lag_body(*refs):
        lag_kernel(scale, *refs)

    lags_of = call(
        lag_body,
        (
            jax.ShapeDtypeStruct((length // 128, 1, 128), F32),
            jax.ShapeDtypeStruct((1, 128), jnp.int32),
        ),
        work,
        size + BLK * length * 8,
        (VMEM, VMEM),
        in_specs=[VMEM],
        scratch_shapes=[
            pltpu.VMEM((128, pieces * CPG), BF16),
            pltpu.VMEM((pieces * CPG + 128, 256), BF16),
            pltpu.VMEM((128, length + 128), F32),
        ],
        name="lags",
    )
    lags, me = lags_of(owned)
    last = halve(lags, me, replicas)
    wide = jax.ShapeDtypeStruct((pos, channels), BF16)
    close = call(
        close_kernel,
        (wide,) * 4 + (jax.ShapeDtypeStruct((1, 128), F32),),
        4 * pos * channels,
        5 * size,
        (ANY,) * 5,
        in_specs=[VMEM] * 7,
        scratch_shapes=[
            pltpu.VMEM((4, pos, channels), BF16),
            pltpu.VMEM((1, 128), F32),
            DMA((PARTS, 4)),
            DMA,
        ],
        name="close",
    )
    *outs, grad_filter = close(back, *flat, *last)
    return tuple(o.reshape(seqcount, pos, channels) for o in outs) + (grad_filter,)


def solution(mesh):
    spread = P("dp", "ctx", None)
    return jax.shard_map(
        step,
        mesh=mesh,
        in_specs=(spread,) * 4 + (P("ctx", None),),
        out_specs=(spread,) * 4 + (P("ctx", "dp"),),
        check_vma=False,
    )
```
